128 devices in a mesh: dp: 32 (over x_lo, z, y), tensor: 4 (over x_hi, core).
Axes of the slice: x: 4 (x_hi: 2, x_lo: 2; x = x_hi * 2 + x_lo), y: 4, z: 4, core: 2. Of those that a mesh axis runs over, the one named last changes fastest.
Arguments:
- inputs: bfloat16 [8192, 1024], P('dp'), may hold values from -6 to 6
- segments: int32 [32, 256], P('dp'), may hold values from 0 to 3, as said below
- positions: int32 [32, 256], P('dp'), may hold values from 0 to 127, as said below
- w_query: bfloat16 [2, 1024, 2048], P(None, None, 'tensor'), may hold values from -0.1875 to 0.1875
- key_weight: bfloat16 [2, 1024, 1024], P(None, None, 'tensor'), may hold values from -0.1875 to 0.1875
- value_weight: bfloat16 [2, 1024, 1024], P(None, None, 'tensor'), may hold values from -0.1875 to 0.1875
- w_out: bfloat16 [2, 2048, 1024], P(None, 'tensor'), may hold values from -0.75 to 0.75
- w_gate: bfloat16 [2, 1024, 3072], P(None, None, 'tensor'), may hold values from -0.1875 to 0.1875
- w_up: bfloat16 [2, 1024, 3072], P(None, None, 'tensor'), may hold values from -0.1875 to 0.1875
- w_down: bfloat16 [2, 3072, 1024], P(None, 'tensor'), may hold values from -0.109375 to 0.109375
- gain_in: float32 [2, 1024], replicated, may hold values from 0.25 to 1.75
- gain_post: float32 [2, 1024], replicated, may hold values from 0.25 to 1.75
- gain_query: float32 [2, 128], replicated, may hold values from 0.5 to 2
- gain_key: float32 [2, 128], replicated, may hold values from 0.5 to 2
- cotangent: bfloat16 [8192, 1024], P('dp'), may hold values from -1.5 to 1.5
Outputs:
- block_out: float32 [8192, 1024], P('dp')
- input_grad: float32 [8192, 1024], P('dp')
- grad_w_query: float32 [2, 1024, 2048], P(None, 'dp', 'tensor')
- grad_w_key: float32 [2, 1024, 1024], P(None, 'dp', 'tensor')
- grad_w_value: float32 [2, 1024, 1024], P(None, 'dp', 'tensor')
- grad_w_out: float32 [2, 2048, 1024], P(None, 'tensor', 'dp')
- grad_w_gate: float32 [2, 1024, 3072], P(None, 'dp', 'tensor')
- grad_w_up: float32 [2, 1024, 3072], P(None, 'dp', 'tensor')
- grad_w_down: float32 [2, 3072, 1024], P(None, 'tensor', 'dp')
- grad_gain_in: float32 [2, 1024], P(None, 'dp')
- grad_gain_post: float32 [2, 1024], P(None, 'dp')
- grad_gain_query: float32 [2, 128], P(None, 'dp')
- grad_gain_key: float32 [2, 128], P(None, 'dp')
The draws below stay inside these ranges and needn't reach their ends.
Inputs may be any that keep to these rules, and one draw needn't show every extreme that they name: `segments`: along each packed row the segment numbers start at 0, never fall, and take exactly four values; every segment holds at most 128 tokens, and in every row one segment holds exactly that many. `positions`: each token's index within its segment, 0 at a segment's first token.
All inputs are finite; a program needn't handle non-finite values.
Results may differ from the reference program's by a relative error of at most 0.025.
Values sent between devices are 32-bit elements; how exact they have to be, the bound alone decides.
No kernel may reach another device: no remote copies, remote signals or barrier semaphores. Data moves between devices by JAX's collectives and lax.ppermute only.
A program may use at most 192 MiB of HBM per device.

```python
import math
import jax
import jax.numpy as jnp
from jax import lax

MODEL_WIDTH = 1024
HQ = 16
KEY_VALUE_HEADS = 8
HEAD_SIZE = 128
FF = 3072
ROW_LEN = 256
DECODER_LAYERS = 2
ROWS = 32
TOKENS = 8192


def segment_layout(key):
    longest = ROW_LEN // 2
    first_key, second_key, slot_key = jax.random.split(jax.random.fold_in(key, 7), 3)
    first_cut = jax.random.randint(first_key, (ROWS, 1), 1, longest).astype(jnp.int32)
    second_cut = jax.random.randint(second_key, (ROWS, 1), 1, longest - 1).astype(jnp.int32)
    second_cut = second_cut + (second_cut >= first_cut).astype(jnp.int32)
    lower_cut = jnp.minimum(first_cut, second_cut)
    upper_cut = jnp.maximum(first_cut, second_cut)
    pieces = jnp.concatenate([lower_cut, upper_cut - lower_cut, longest - upper_cut], axis=1)
    zero_col = jnp.zeros((ROWS, 1), jnp.int32)
    before = jnp.concatenate([pieces, zero_col], axis=1)
    after = jnp.concatenate([zero_col, pieces], axis=1)
    slot = jax.random.randint(slot_key, (ROWS, 1), 0, 4).astype(jnp.int32)
    slot_ids = jnp.arange(4, dtype=jnp.int32)[None, :]
    lengths = jnp.where(slot_ids < slot, before, jnp.where(slot_ids == slot, longest, after)).astype(jnp.int32)
    ends = jnp.cumsum(lengths, axis=1).astype(jnp.int32)
    bounds = ends[:, :3]
    column_ids = jnp.arange(ROW_LEN, dtype=jnp.int32)[None, :]
    segment_ids = jnp.sum((column_ids[:, :, None] >= bounds[:, None, :]).astype(jnp.int32), axis=2).astype(jnp.int32)
    starts = jnp.concatenate([zero_col, bounds], axis=1)
    segment_start = jnp.sum(jnp.where(segment_ids[:, :, None] == slot_ids[:, None, :], starts[:, None, :], 0), axis=2).astype(jnp.int32)
    return (segment_ids, (column_ids - segment_start).astype(jnp.int32))


def draw_segments(key, part):
    return segment_layout(key)[0]


def draw_positions(key, part):
    return segment_layout(key)[1]


def with_spikes(entries, stream_key, source, target, shards_of, factor):
    def block_of(axis_at):
        return (jnp.arange(entries.shape[axis_at]) // (entries.shape[axis_at] // shards_of)).reshape((-1,) + (1,) * (entries.ndim - 1 - axis_at))

    near = jax.random.permutation(stream_key, shards_of)[block_of(target)]
    other_side = (block_of(target) + shards_of // 2) % shards_of
    return jnp.where((block_of(source) == near) | (block_of(source) == other_side), factor * entries, entries)


def block_scale(rng, dims, cuts, smallest, high):
    level = 1.0
    for axis_at, blocks in cuts:
        draws = jax.random.uniform(jax.random.fold_in(jax.random.fold_in(rng, 6), axis_at), (blocks,), jnp.float32, smallest / len(cuts), high / len(cuts))
        level = level * jnp.repeat(jnp.exp(draws), dims[axis_at] // blocks).reshape((-1,) + (1,) * (len(dims) - 1 - axis_at))
    return level


def centred(own_key, shape, scale, reach, shards=(), kind=jnp.bfloat16):
    level = block_scale(own_key, shape, shards, -0.22, 0.18) if shards else 1.0
    values = jax.random.normal(own_key, shape, jnp.float32) * scale * level
    return jnp.minimum(jnp.maximum(values, -reach), reach).astype(kind)


def noise_with(key, dims, deviation, reach, cuts, heavy, kind=jnp.bfloat16):
    values = deviation * jax.random.normal(key, dims, jnp.float32)
    if cuts:
        values = values * block_scale(key, dims, cuts, -0.22, 0.18)
    return jnp.clip(with_spikes(values, jax.random.fold_in(key, 3), *heavy), -reach, reach).astype(kind)


def setup_inputs(seed: int = 0) -> dict:
    streams_of = jax.random.split(jax.random.key(seed), 16)
    return {
        "inputs": centred(streams_of[0], (TOKENS, MODEL_WIDTH), 1.0, 6.0, ((0, 32),)),
        "segments": draw_segments(jax.random.fold_in(streams_of[15], 71), 0),
        "positions": draw_positions(jax.random.fold_in(streams_of[15], 71), 0),
        "w_query": centred(streams_of[3], (DECODER_LAYERS, MODEL_WIDTH, HQ * HEAD_SIZE), MODEL_WIDTH ** -0.5, 0.1875, ((2, 4),)),
        "key_weight": centred(streams_of[4], (DECODER_LAYERS, MODEL_WIDTH, KEY_VALUE_HEADS * HEAD_SIZE), MODEL_WIDTH ** -0.5, 0.1875, ((2, 4),)),
        "value_weight": centred(streams_of[5], (DECODER_LAYERS, MODEL_WIDTH, KEY_VALUE_HEADS * HEAD_SIZE), MODEL_WIDTH ** -0.5, 0.1875, ((2, 4),)),
        "w_out": centred(streams_of[6], (DECODER_LAYERS, HQ * HEAD_SIZE, MODEL_WIDTH), (HQ * HEAD_SIZE // 32) ** -0.5, 0.75, ((1, 4),)),
        "w_gate": centred(streams_of[7], (DECODER_LAYERS, MODEL_WIDTH, FF), MODEL_WIDTH ** -0.5, 0.1875, ((2, 4),)),
        "w_up": centred(streams_of[8], (DECODER_LAYERS, MODEL_WIDTH, FF), MODEL_WIDTH ** -0.5, 0.1875, ((2, 4),)),
        "w_down": centred(streams_of[9], (DECODER_LAYERS, FF, MODEL_WIDTH), FF ** -0.5, 0.109375, ((1, 4),)),
        "gain_in": jnp.clip(1.0 + 0.15 * jax.random.normal(streams_of[10], (DECODER_LAYERS, MODEL_WIDTH), jnp.float32), 0.25, 1.75),
        "gain_post": jnp.clip(1.0 + 0.15 * jax.random.normal(streams_of[11], (DECODER_LAYERS, MODEL_WIDTH), jnp.float32), 0.25, 1.75),
        "gain_query": jnp.clip(jnp.exp(jax.random.uniform(streams_of[12], (DECODER_LAYERS, HEAD_SIZE), jnp.float32, math.log(0.5), math.log(2.0))), 0.5, 2.0),
        "gain_key": jnp.clip(jnp.exp(jax.random.uniform(streams_of[13], (DECODER_LAYERS, HEAD_SIZE), jnp.float32, math.log(0.5), math.log(2.0))), 0.5, 2.0),
        "cotangent": noise_with(streams_of[14], (TOKENS, MODEL_WIDTH), 0.25, 1.5, ((0, 32),), (0, 1, 32, 2.75)),
    }


EPS = 1e-06
THETA = 1000000.0
NEG_FILL = -1e+30

def inv_rms(values):
    return lax.rsqrt(lax.optimization_barrier(jnp.mean(values * values, axis=-1, keepdims=True)) + EPS)

def norm_back(upstream, normed, scale_inv, gain):
    scaled = upstream * gain
    return scale_inv * (scaled - normed * lax.optimization_barrier(jnp.mean(scaled * normed, axis=-1, keepdims=True)))

def rope_tables(position_ids, head_dim):
    half_dim = head_dim // 2
    inverse_freq = THETA ** (-(jnp.arange(half_dim).astype(jnp.float32) * 2.0 / head_dim))
    angles = position_ids.astype(jnp.float32)[:, None] * inverse_freq[None, :]
    return (jnp.cos(angles)[:, None, :], jnp.sin(angles)[:, None, :])

def rotate(values, cosine, sine):
    half_dim = values.shape[-1] // 2
    lower_half = values[..., :half_dim]
    upper_half = values[..., half_dim:]
    return jnp.concatenate([lower_half * cosine - upper_half * sine, upper_half * cosine + lower_half * sine], axis=-1)

def rotate_back(values, cosine, sine):
    half_dim = values.shape[-1] // 2
    lower_half = values[..., :half_dim]
    upper_half = values[..., half_dim:]
    return jnp.concatenate([lower_half * cosine + upper_half * sine, upper_half * cosine - lower_half * sine], axis=-1)

def contract(form, left, right):
    return jnp.einsum(form, left.astype(jnp.float32), right.astype(jnp.float32))

def row_scores(q_part, k_rot, segment_row, first_row, score_scale):
    rows_here = q_part.shape[0]
    scores = contract('qkgd,skd->kgqs', q_part, k_rot) * score_scale
    query_ids = first_row + jnp.arange(rows_here)
    key_ids = jnp.arange(k_rot.shape[0])
    allowed = (segment_row[first_row:first_row + rows_here, None] == segment_row[None, :]) & (key_ids[None, :] <= query_ids[:, None])
    return jnp.where(allowed, scores, NEG_FILL)

def attention_forward(q_rot, k_rot, values, segment_row):
    length, kv_heads, head_dim = k_rot.shape
    groups = q_rot.shape[1] // kv_heads
    block_rows = min(512, length)
    score_scale = head_dim ** (-0.5)
    outputs = []
    totals = []
    for first_row in range(0, length, block_rows):
        q_part = q_rot[first_row:first_row + block_rows].reshape(block_rows, kv_heads, groups, head_dim)
        scores = row_scores(q_part, k_rot, segment_row, first_row, score_scale)
        row_peak = lax.optimization_barrier(jnp.max(scores, axis=-1, keepdims=True))
        log_total = row_peak + jnp.log(lax.optimization_barrier(jnp.sum(jnp.exp(scores - row_peak), axis=-1, keepdims=True)))
        weights = jnp.exp(scores - log_total).astype(jnp.bfloat16)
        attended = contract('kgqs,skd->qkgd', weights, values)
        outputs.append(attended.reshape(block_rows, -1).astype(jnp.bfloat16))
        totals.append(log_total)
    return (jnp.concatenate(outputs, axis=0), jnp.concatenate(totals, axis=2))

def attention_backward(q_rot, k_rot, values, attended, grad_attended, log_totals, segment_row):
    length, kv_heads, head_dim = k_rot.shape
    groups = q_rot.shape[1] // kv_heads
    block_rows = min(512, length)
    score_scale = head_dim ** (-0.5)
    grad_keys = jnp.zeros((length, kv_heads, head_dim), jnp.float32)
    grad_values = jnp.zeros((length, kv_heads, head_dim), jnp.float32)
    grad_queries = []
    for first_row in range(0, length, block_rows):
        q_part = q_rot[first_row:first_row + block_rows].reshape(block_rows, kv_heads, groups, head_dim)
        go_part = grad_attended[first_row:first_row + block_rows].reshape(block_rows, kv_heads, groups, head_dim)
        o_part = attended[first_row:first_row + block_rows].reshape(block_rows, kv_heads, groups, head_dim)
        scores = row_scores(q_part, k_rot, segment_row, first_row, score_scale)
        probs = jnp.exp(scores - log_totals[:, :, first_row:first_row + block_rows])
        weights = probs.astype(jnp.bfloat16)
        grad_values = grad_values + contract('kgqs,qkgd->skd', weights, go_part)
        grad_probs = contract('qkgd,skd->kgqs', go_part, values)
        row_dots = contract('qkgd,qkgd->kgq', go_part, o_part)
        grad_scores = (probs * (grad_probs - row_dots[..., None]) * score_scale).astype(jnp.bfloat16)
        grad_queries.append(contract('kgqs,skd->qkgd', grad_scores, k_rot).reshape(block_rows, kv_heads * groups, head_dim))
        grad_keys = grad_keys + contract('kgqs,qkgd->skd', grad_scores, q_part)
    return (jnp.concatenate(grad_queries, axis=0), grad_keys, grad_values)

def forward_layer(resid, segments, cosine, sine, params):
    w_query, key_weight, value_weight, w_out, w_gate, w_up, w_down, gain_in, gain_post, gain_query, gain_key = params
    token_count = resid.shape[0]
    row_count = segments.shape[0]
    row_len = segments.shape[1]
    head_dim = gain_query.shape[0]
    scale_in = inv_rms(resid)
    normed_in = resid * scale_in
    attn_input = (normed_in * gain_in).astype(jnp.bfloat16)
    queries = jnp.dot(attn_input, w_query, preferred_element_type=jnp.float32).reshape(token_count, -1, head_dim)
    keys_raw = jnp.dot(attn_input, key_weight, preferred_element_type=jnp.float32).reshape(token_count, -1, head_dim)
    values = jnp.dot(attn_input, value_weight, preferred_element_type=jnp.float32).astype(jnp.bfloat16).reshape(token_count, -1, head_dim)
    q_scale = inv_rms(queries)
    q_normed = queries * q_scale
    k_scale = inv_rms(keys_raw)
    k_normed = keys_raw * k_scale
    q_rot = rotate(q_normed * gain_query, cosine, sine).astype(jnp.bfloat16)
    k_rot = rotate(k_normed * gain_key, cosine, sine).astype(jnp.bfloat16)

    def per_row(pieces):
        return attention_forward(pieces[0], pieces[1], pieces[2], pieces[3])
    attended, log_totals = lax.map(per_row, (q_rot.reshape(row_count, row_len, -1, head_dim), k_rot.reshape(row_count, row_len, -1, head_dim), values.reshape(row_count, row_len, -1, head_dim), segments))
    attended = attended.reshape(token_count, -1)
    middle = resid + jnp.dot(attended, w_out, preferred_element_type=jnp.float32)
    scale_post = inv_rms(middle)
    normed_post = middle * scale_post
    mlp_input = (normed_post * gain_post).astype(jnp.bfloat16)
    gate_logits = jnp.dot(mlp_input, w_gate, preferred_element_type=jnp.float32)
    up_pre = jnp.dot(mlp_input, w_up, preferred_element_type=jnp.float32)
    hidden = (jax.nn.silu(gate_logits) * up_pre).astype(jnp.bfloat16)
    result = middle + jnp.dot(hidden, w_down, preferred_element_type=jnp.float32)
    saved = (scale_in, normed_in, attn_input, q_scale, q_normed, k_scale, k_normed, q_rot, k_rot, values, attended, log_totals, scale_post, normed_post, mlp_input, gate_logits, up_pre, hidden)
    return (result, saved)

def backward_layer(upstream, saved, params, segments, cosine, sine):
    w_query, key_weight, value_weight, w_out, w_gate, w_up, w_down, gain_in, gain_post, gain_query, gain_key = params
    scale_in, normed_in, attn_input, q_scale, q_normed, k_scale, k_normed, q_rot, k_rot, values, attended, log_totals, scale_post, normed_post, mlp_input, gate_logits, up_pre, hidden = saved
    token_count = upstream.shape[0]
    row_count = segments.shape[0]
    row_len = segments.shape[1]
    head_dim = gain_query.shape[0]
    upstream_bf = upstream.astype(jnp.bfloat16)
    grad_down = jnp.dot(hidden.T, upstream_bf, preferred_element_type=jnp.float32)
    grad_hidden = jnp.dot(upstream_bf, w_down.T, preferred_element_type=jnp.float32)
    sigma = jax.nn.sigmoid(gate_logits)
    grad_gate_pre = (grad_hidden * up_pre * sigma * (1.0 + gate_logits * (1.0 - sigma))).astype(jnp.bfloat16)
    grad_up_pre = (grad_hidden * gate_logits * sigma).astype(jnp.bfloat16)
    grad_gate = jnp.dot(mlp_input.T, grad_gate_pre, preferred_element_type=jnp.float32)
    grad_upward = jnp.dot(mlp_input.T, grad_up_pre, preferred_element_type=jnp.float32)
    grad_mlp_in = jnp.dot(grad_gate_pre, w_gate.T, preferred_element_type=jnp.float32) + jnp.dot(grad_up_pre, w_up.T, preferred_element_type=jnp.float32)
    grad_gain_post = lax.optimization_barrier(jnp.sum(grad_mlp_in * normed_post, axis=0))
    grad_middle = upstream + norm_back(grad_mlp_in, normed_post, scale_post, gain_post)
    middle_bf = grad_middle.astype(jnp.bfloat16)
    grad_output = jnp.dot(attended.T, middle_bf, preferred_element_type=jnp.float32)
    grad_attended = jnp.dot(middle_bf, w_out.T, preferred_element_type=jnp.float32).astype(jnp.bfloat16)

    def per_row(pieces):
        return attention_backward(pieces[0], pieces[1], pieces[2], pieces[3], pieces[4], pieces[5], pieces[6])
    grad_q_rot, grad_k_rot, grad_v_raw = lax.map(per_row, (q_rot.reshape(row_count, row_len, -1, head_dim), k_rot.reshape(row_count, row_len, -1, head_dim), values.reshape(row_count, row_len, -1, head_dim), attended.reshape(row_count, row_len, -1), grad_attended.reshape(row_count, row_len, -1), log_totals, segments))
    grad_q_rot = grad_q_rot.reshape(token_count, -1, head_dim)
    grad_k_rot = grad_k_rot.reshape(token_count, -1, head_dim)
    grad_q_normed = rotate_back(grad_q_rot, cosine, sine)
    grad_k_normed = rotate_back(grad_k_rot, cosine, sine)
    grad_gain_query = lax.optimization_barrier(jnp.sum(grad_q_normed * q_normed, axis=(0, 1)))
    grad_gain_key = lax.optimization_barrier(jnp.sum(grad_k_normed * k_normed, axis=(0, 1)))
    grad_queries = norm_back(grad_q_normed, q_normed, q_scale, gain_query).astype(jnp.bfloat16).reshape(token_count, -1)
    grad_keys = norm_back(grad_k_normed, k_normed, k_scale, gain_key).astype(jnp.bfloat16).reshape(token_count, -1)
    grad_values = grad_v_raw.astype(jnp.bfloat16).reshape(token_count, -1)
    query_gradient = jnp.dot(attn_input.T, grad_queries, preferred_element_type=jnp.float32)
    grad_key = jnp.dot(attn_input.T, grad_keys, preferred_element_type=jnp.float32)
    grad_value = jnp.dot(attn_input.T, grad_values, preferred_element_type=jnp.float32)
    grad_attn_in = jnp.dot(grad_queries, w_query.T, preferred_element_type=jnp.float32) + jnp.dot(grad_keys, key_weight.T, preferred_element_type=jnp.float32) + jnp.dot(grad_values, value_weight.T, preferred_element_type=jnp.float32)
    grad_gain_in = lax.optimization_barrier(jnp.sum(grad_attn_in * normed_in, axis=0))
    grad_resid = grad_middle + norm_back(grad_attn_in, normed_in, scale_in, gain_in)
    return (grad_resid, (query_gradient, grad_key, grad_value, grad_output, grad_gate, grad_upward, grad_down, grad_gain_in, grad_gain_post, grad_gain_query, grad_gain_key))

def reference(inputs, segments, positions, w_query, key_weight, value_weight, w_out, w_gate, w_up, w_down, gain_in, gain_post, gain_query, gain_key, cotangent):
    all_params = (w_query, key_weight, value_weight, w_out, w_gate, w_up, w_down, gain_in, gain_post, gain_query, gain_key)
    layer_count = w_query.shape[0]
    cosine, sine = rope_tables(positions.reshape(-1), gain_query.shape[1])
    resid = inputs.astype(jnp.float32)
    saves = []
    for layer_idx in range(layer_count):
        params = tuple((member[layer_idx] for member in all_params))
        resid, saved = forward_layer(resid, segments, cosine, sine, params)
        saves.append(saved)
    result = resid
    upstream = cotangent.astype(jnp.float32)
    collected = []
    for layer_idx in reversed(range(layer_count)):
        params = tuple((member[layer_idx] for member in all_params))
        upstream, layer_terms = backward_layer(upstream, saves[layer_idx], params, segments, cosine, sine)
        collected.insert(0, layer_terms)
    stacked = tuple((jnp.stack([layer_terms[member_idx] for layer_terms in collected]) for member_idx in range(11)))
    return (result, upstream, stacked[0], stacked[1], stacked[2], stacked[3], stacked[4], stacked[5], stacked[6], stacked[7], stacked[8], stacked[9], stacked[10])
```

```python
import jax
import jax.numpy as jnp
from jax import lax
from jax.experimental import pallas as pl
from jax.experimental.pallas import tpu as pltpu
from jax.sharding import Mesh, PartitionSpec as P

EPS = 1e-06
THETA = 1000000.0
NEG_FILL = -1e30


def inv_rms(values):
    return lax.rsqrt(jnp.mean(values * values, axis=-1, keepdims=True) + EPS)


def norm_back(upstream, normed, scale_inv, gain):
    scaled = upstream * gain
    return scale_inv * (scaled - normed * jnp.mean(scaled * normed, axis=-1, keepdims=True))


def rope_tables(position_ids, head_dim):
    half_dim = head_dim // 2
    inverse_freq = THETA ** (-(jnp.arange(half_dim).astype(jnp.float32) * 2.0 / head_dim))
    angles = position_ids.astype(jnp.float32)[:, None] * inverse_freq[None, :]
    return (jnp.cos(angles)[:, None, :], jnp.sin(angles)[:, None, :])


def rotate(values, cosine, sine):
    half_dim = values.shape[-1] // 2
    lower_half = values[..., :half_dim]
    upper_half = values[..., half_dim:]
    return jnp.concatenate(
        [lower_half * cosine - upper_half * sine, upper_half * cosine + lower_half * sine], axis=-1
    )


def rotate_back(values, cosine, sine):
    half_dim = values.shape[-1] // 2
    lower_half = values[..., :half_dim]
    upper_half = values[..., half_dim:]
    return jnp.concatenate(
        [lower_half * cosine + upper_half * sine, upper_half * cosine - lower_half * sine], axis=-1
    )


def contract(form, left, right):
    return jnp.einsum(form, left, right, preferred_element_type=jnp.float32)


SWAP = ((0, 1), (1, 0))


def row_scores(q_part, k_rot, allowed, score_scale):
    scores = contract("qkgd,skd->kgqs", q_part, k_rot) * score_scale
    return jnp.where(allowed, scores, NEG_FILL)


def attention_forward(q_rot, k_rot, values, allowed):
    length, kv_heads, head_dim = k_rot.shape
    groups = q_rot.shape[1] // kv_heads
    score_scale = head_dim ** (-0.5)
    q_part = q_rot.reshape(length, kv_heads, groups, head_dim)
    scores = row_scores(q_part, k_rot, allowed, score_scale)
    row_peak = jnp.max(scores, axis=-1, keepdims=True)
    log_total = row_peak + jnp.log(jnp.sum(jnp.exp(scores - row_peak), axis=-1, keepdims=True))
    probs = jnp.exp(scores - log_total)
    attended = contract("kgqs,skd->qkgd", probs.astype(jnp.bfloat16), values)
    outputs = attended.reshape(length, -1).astype(jnp.bfloat16)
    return (outputs, log_total)


def attention_backward(q_rot, k_rot, values, attended, grad_attended, log_totals, allowed):
    length, kv_heads, head_dim = k_rot.shape
    groups = q_rot.shape[1] // kv_heads
    score_scale = head_dim ** (-0.5)
    q_part = q_rot.reshape(length, kv_heads, groups, head_dim)
    go_part = grad_attended.reshape(length, kv_heads, groups, head_dim)
    o_part = attended.reshape(length, kv_heads, groups, head_dim)
    scores = row_scores(q_part, k_rot, allowed, score_scale)
    probs = jnp.exp(scores - log_totals)
    weights = probs.astype(jnp.bfloat16)
    grad_values = contract("kgqs,qkgd->skd", weights, go_part)
    grad_probs = contract("qkgd,skd->kgqs", go_part, values)
    row_dots = contract("qkgd,qkgd->kgq", go_part, o_part)
    grad_scores = (probs * (grad_probs - row_dots[..., None]) * score_scale).astype(jnp.bfloat16)
    grad_queries = contract("kgqs,skd->qkgd", grad_scores, k_rot).reshape(
        length, kv_heads * groups, head_dim
    )
    grad_keys = contract("kgqs,qkgd->skd", grad_scores, q_part)
    return (grad_queries, grad_keys, grad_values)


def group_sum(partial):
    half = partial.shape[0] // 2
    own = partial[:half] + lax.ppermute(partial[half:], "core", SWAP)
    own = own + lax.ppermute(own, "x_hi", SWAP)
    return jnp.concatenate([own, lax.ppermute(own, "core", SWAP)], axis=0)


def weight_grads(pairs):
    tokens, width = pairs[0][0].shape
    lefts = []
    for left, _ in pairs:
        if not any(left is seen for seen in lefts):
            lefts.append(left)
    which = [next(i for i, seen in enumerate(lefts) if seen is left) for left, _ in pairs]
    rights = [right for _, right in pairs]
    columns = [right.shape[1] for right in rights]
    total = sum(columns)
    n_left = len(lefts)
    tile = 256
    halves = width // 2
    per_half = halves // tile

    def body(*refs):
        left_refs = refs[:n_left]
        right_refs = refs[n_left:-1]
        out_ref = refs[-1]
        start = 0
        for idx, right_ref in enumerate(right_refs):
            piece = lax.dot_general(
                left_refs[which[idx]][...],
                right_ref[...],
                (((0,), (0,)), ((), ())),
                preferred_element_type=jnp.float32,
            )
            out_ref[:, 0, :, start : start + columns[idx]] = piece.reshape(
                tile // 32, 32, columns[idx]
            )
            start += columns[idx]

    flops = 2 * tokens * width * total
    out = pl.pallas_call(
        body,
        grid=(2 * per_half,),
        in_specs=[pl.BlockSpec((tokens, tile), lambda i: (0, i)) for _ in lefts]
        + [pl.BlockSpec((tokens, c), lambda i: (0, 0)) for c in columns],
        out_specs=pl.BlockSpec(
            (tile // 32, 1, 32, total), lambda i: (i % per_half, i // per_half, 0, 0)
        ),
        out_shape=jax.ShapeDtypeStruct((width // 64, 2, 32, total), jnp.float32),
        cost_estimate=pl.CostEstimate(
            flops=flops, transcendentals=0, bytes_accessed=4 * width * total
        ),
        name="weight_grads",
    )(*lefts, *rights)
    return out.reshape(width, total)


def scatter_rows(stacked):
    part = lax.psum_scatter(stacked, ("z", "y"), scatter_dimension=0, tiled=True)
    rows = part.shape[0] // 2
    part = part.reshape(2, rows, part.shape[1])
    mine = lax.axis_index("x_lo")
    keep = lax.dynamic_index_in_dim(part, mine, 0, keepdims=False)
    send = lax.dynamic_index_in_dim(part, 1 - mine, 0, keepdims=False)
    return keep + lax.ppermute(send, "x_lo", SWAP)


def sum_everywhere(small):
    for axis in ("x_lo", "y", "z"):
        size = lax.axis_size(axis)
        step = 1
        while step < size:
            small = small + lax.ppermute(small, axis, [(i, i ^ step) for i in range(size)])
            step *= 2
    for axis in ("core", "x_hi"):
        small = small + lax.ppermute(small, axis, SWAP)
    return small


def layer_forward(resid, allowed, cosine, sine, params):
    (w_query, key_weight, value_weight, w_out, w_gate, w_up, w_down) = params[:7]
    (gain_in, gain_post, gain_query, gain_key) = params[7:]
    length = resid.shape[0]
    head_dim = gain_query.shape[0]
    scale_in = inv_rms(resid)
    normed_in = resid * scale_in
    attn_input = (normed_in * gain_in).astype(jnp.bfloat16)
    queries = jnp.dot(attn_input, w_query, preferred_element_type=jnp.float32).reshape(
        length, -1, head_dim
    )
    keys_raw = jnp.dot(attn_input, key_weight, preferred_element_type=jnp.float32).reshape(
        length, -1, head_dim
    )
    values = (
        jnp.dot(attn_input, value_weight, preferred_element_type=jnp.float32)
        .astype(jnp.bfloat16)
        .reshape(length, -1, head_dim)
    )
    q_scale = inv_rms(queries)
    q_normed = queries * q_scale
    k_scale = inv_rms(keys_raw)
    k_normed = keys_raw * k_scale
    q_rot = rotate(q_normed * gain_query, cosine, sine).astype(jnp.bfloat16)
    k_rot = rotate(k_normed * gain_key, cosine, sine).astype(jnp.bfloat16)
    attended, log_totals = attention_forward(q_rot, k_rot, values, allowed)
    attn_sum = group_sum(jnp.dot(attended, w_out, preferred_element_type=jnp.float32))
    middle = resid + attn_sum
    scale_post = inv_rms(middle)
    normed_post = middle * scale_post
    mlp_input = (normed_post * gain_post).astype(jnp.bfloat16)
    gate_logits = jnp.dot(mlp_input, w_gate, preferred_element_type=jnp.float32)
    up_pre = jnp.dot(mlp_input, w_up, preferred_element_type=jnp.float32)
    hidden = (jax.nn.silu(gate_logits) * up_pre).astype(jnp.bfloat16)
    mlp_sum = group_sum(jnp.dot(hidden, w_down, preferred_element_type=jnp.float32))
    result = middle + mlp_sum
    saved = (
        scale_in,
        normed_in,
        attn_input,
        q_scale,
        q_normed,
        k_scale,
        k_normed,
        q_rot,
        k_rot,
        values,
        attended,
        log_totals,
        scale_post,
        normed_post,
        mlp_input,
        gate_logits,
        up_pre,
        hidden,
    )
    return (result, saved)


def layer_backward(upstream, saved, params, allowed, cosine, sine):
    (w_query, key_weight, value_weight, w_out, w_gate, w_up, w_down) = params[:7]
    (gain_in, gain_post, gain_query, gain_key) = params[7:]
    (
        scale_in,
        normed_in,
        attn_input,
        q_scale,
        q_normed,
        k_scale,
        k_normed,
        q_rot,
        k_rot,
        values,
        attended,
        log_totals,
        scale_post,
        normed_post,
        mlp_input,
        gate_logits,
        up_pre,
        hidden,
    ) = saved
    length = upstream.shape[0]
    upstream_bf = upstream.astype(jnp.bfloat16)
    grad_hidden = jnp.dot(upstream_bf, w_down.T, preferred_element_type=jnp.float32)
    sigma = jax.nn.sigmoid(gate_logits)
    grad_gate_pre = (grad_hidden * up_pre * sigma * (1.0 + gate_logits * (1.0 - sigma))).astype(
        jnp.bfloat16
    )
    grad_up_pre = (grad_hidden * gate_logits * sigma).astype(jnp.bfloat16)
    mlp_partial = jnp.dot(grad_gate_pre, w_gate.T, preferred_element_type=jnp.float32) + jnp.dot(
        grad_up_pre, w_up.T, preferred_element_type=jnp.float32
    )
    grad_mlp_in = group_sum(mlp_partial)
    mlp_grads = scatter_rows(
        weight_grads(
            [(mlp_input, grad_gate_pre), (mlp_input, grad_up_pre), (upstream_bf, hidden)]
        )
    )
    grad_gain_post = jnp.sum(mlp_partial * normed_post, axis=0)
    grad_middle = upstream + norm_back(grad_mlp_in, normed_post, scale_post, gain_post)
    middle_bf = grad_middle.astype(jnp.bfloat16)
    grad_attended = jnp.dot(middle_bf, w_out.T, preferred_element_type=jnp.float32).astype(
        jnp.bfloat16
    )
    grad_q_rot, grad_k_rot, grad_v_raw = attention_backward(
        q_rot, k_rot, values, attended, grad_attended, log_totals, allowed
    )
    grad_q_normed = rotate_back(grad_q_rot, cosine, sine)
    grad_k_normed = rotate_back(grad_k_rot, cosine, sine)
    query_gain_part = jnp.sum(grad_q_normed * q_normed, axis=(0, 1))
    key_gain_part = jnp.sum(grad_k_normed * k_normed, axis=(0, 1))
    grad_queries = (
        norm_back(grad_q_normed, q_normed, q_scale, gain_query)
        .astype(jnp.bfloat16)
        .reshape(length, -1)
    )
    grad_keys = (
        norm_back(grad_k_normed, k_normed, k_scale, gain_key)
        .astype(jnp.bfloat16)
        .reshape(length, -1)
    )
    grad_values = grad_v_raw.astype(jnp.bfloat16).reshape(length, -1)
    attn_partial = (
        jnp.dot(grad_queries, w_query.T, preferred_element_type=jnp.float32)
        + jnp.dot(grad_keys, key_weight.T, preferred_element_type=jnp.float32)
        + jnp.dot(grad_values, value_weight.T, preferred_element_type=jnp.float32)
    )
    attn_grads = scatter_rows(
        weight_grads(
            [
                (attn_input, grad_queries),
                (attn_input, grad_keys),
                (attn_input, grad_values),
                (middle_bf, attended),
            ]
        )
    )
    grad_attn_in = group_sum(attn_partial)
    grad_gain_in = jnp.sum(attn_partial * normed_in, axis=0)
    grad_resid = grad_middle + norm_back(grad_attn_in, normed_in, scale_in, gain_in)
    gains = (grad_gain_in, grad_gain_post, query_gain_part, key_gain_part)
    return (grad_resid, mlp_grads, attn_grads, gains)


def split_columns(stacked, sizes):
    pieces = []
    start = 0
    for size in sizes:
        pieces.append(stacked[:, start : start + size])
        start += size
    return pieces


def shards(
    inputs,
    segments,
    positions,
    w_query,
    key_weight,
    value_weight,
    w_out,
    w_gate,
    w_up,
    w_down,
    gain_in,
    gain_post,
    gain_query,
    gain_key,
    cotangent,
):
    all_params = (
        w_query,
        key_weight,
        value_weight,
        w_out,
        w_gate,
        w_up,
        w_down,
        gain_in,
        gain_post,
        gain_query,
        gain_key,
    )
    layer_count = w_query.shape[0]
    length = segments.shape[1]
    width = inputs.shape[1]
    half = length // 2
    core = lax.axis_index("core")

    def turn(values):
        return jnp.where(core == 0, values, jnp.concatenate([values[half:], values[:half]], axis=0))

    segment_row = turn(segments[0])
    index_row = turn(jnp.arange(length))
    allowed = (segment_row[:, None] == segment_row[None, :]) & (
        index_row[None, :] <= index_row[:, None]
    )
    cosine, sine = rope_tables(turn(positions[0]), gain_query.shape[1])
    resid = turn(inputs).astype(jnp.float32)
    saves = []
    for layer_idx in range(layer_count):
        params = tuple((member[layer_idx] for member in all_params))
        resid, saved = layer_forward(resid, allowed, cosine, sine, params)
        saves.append(saved)
    upstream = turn(cotangent).astype(jnp.float32)
    mlp_rows, attn_rows, gains = ([], [], [])
    for layer_idx in reversed(range(layer_count)):
        params = tuple((member[layer_idx] for member in all_params))
        upstream, mlp_part, attn_part, gain_part = layer_backward(
            upstream, saves[layer_idx], params, allowed, cosine, sine
        )
        mlp_rows.insert(0, mlp_part)
        attn_rows.insert(0, attn_part)
        gains.insert(0, gain_part)
    sizes = [member.shape[1] for group in gains for member in [g[None] for g in group]]
    flat = sum_everywhere(
        jnp.concatenate([member for group in gains for member in group]).reshape(-1, 128)
    ).reshape(-1)
    place = lax.axis_index(("x_lo", "z", "y"))
    n_place = lax.axis_size(("x_lo", "z", "y"))
    gain_pieces = []
    start = 0
    for size in sizes:
        piece = flat[start : start + size].reshape(n_place, size // n_place)
        gain_pieces.append(lax.dynamic_index_in_dim(piece, place, 0, keepdims=False))
        start += size
    gain_out = [
        jnp.stack([gain_pieces[4 * layer_idx + member] for layer_idx in range(layer_count)])
        for member in range(4)
    ]
    hidden_here = w_gate.shape[2]
    mlp_split = [split_columns(rows, [hidden_here] * 3) for rows in mlp_rows]
    attn_split = [
        split_columns(
            rows, [w_query.shape[2], key_weight.shape[2], value_weight.shape[2], w_out.shape[1]]
        )
        for rows in attn_rows
    ]
    return (
        turn(resid),
        turn(upstream),
        jnp.stack([pieces[0] for pieces in attn_split]),
        jnp.stack([pieces[1] for pieces in attn_split]),
        jnp.stack([pieces[2] for pieces in attn_split]),
        jnp.stack([pieces[3].T for pieces in attn_split]),
        jnp.stack([pieces[0] for pieces in mlp_split]),
        jnp.stack([pieces[1] for pieces in mlp_split]),
        jnp.stack([pieces[2].T for pieces in mlp_split]),
        gain_out[0],
        gain_out[1],
        gain_out[2],
        gain_out[3],
    )


def solution(mesh):
    fine = Mesh(
        mesh.devices.reshape(2, 4, 4, 2, 2), ("x_lo", "z", "y", "x_hi", "core")
    )
    dp = ("x_lo", "z", "y")
    tensor = ("x_hi", "core")
    return jax.shard_map(
        shards,
        mesh=fine,
        in_specs=(
            P(dp, None),
            P(dp, None),
            P(dp, None),
            P(None, None, tensor),
            P(None, None, tensor),
            P(None, None, tensor),
            P(None, tensor, None),
            P(None, None, tensor),
            P(None, None, tensor),
            P(None, tensor, None),
            P(),
            P(),
            P(),
            P(),
            P(dp, None),
        ),
        out_specs=(
            P(dp, None),
            P(dp, None),
            P(None, dp, tensor),
            P(None, dp, tensor),
            P(None, dp, tensor),
            P(None, tensor, dp),
            P(None, dp, tensor),
            P(None, dp, tensor),
            P(None, tensor, dp),
            P(None, dp),
            P(None, dp),
            P(None, dp),
            P(None, dp),
        ),
        check_vma=False,
    )
```

```python
import jax
import jax.numpy as jnp
from jax import lax
from jax.experimental import pallas as pl
from jax.experimental.pallas import tpu as pltpu
from jax.sharding import Mesh, PartitionSpec as P

EPS = 1e-06
THETA = 1000000.0
NEG_FILL = -1e30


def inv_rms(values):
    return lax.rsqrt(jnp.mean(values * values, axis=-1, keepdims=True) + EPS)


def norm_back(upstream, normed, scale_inv, gain):
    scaled = upstream * gain
    return scale_inv * (scaled - normed * jnp.mean(scaled * normed, axis=-1, keepdims=True))


def rope_tables(position_ids, head_dim):
    half_dim = head_dim // 2
    inverse_freq = THETA ** (-(jnp.arange(half_dim).astype(jnp.float32) * 2.0 / head_dim))
    angles = position_ids.astype(jnp.float32)[:, None] * inverse_freq[None, :]
    return (jnp.cos(angles)[:, None, :], jnp.sin(angles)[:, None, :])


def rotate(values, cosine, sine):
    half_dim = values.shape[-1] // 2
    lower_half = values[..., :half_dim]
    upper_half = values[..., half_dim:]
    return jnp.concatenate(
        [lower_half * cosine - upper_half * sine, upper_half * cosine + lower_half * sine], axis=-1
    )


def rotate_back(values, cosine, sine):
    half_dim = values.shape[-1] // 2
    lower_half = values[..., :half_dim]
    upper_half = values[..., half_dim:]
    return jnp.concatenate(
        [lower_half * cosine + upper_half * sine, upper_half * cosine - lower_half * sine], axis=-1
    )


def contract(form, left, right):
    return jnp.einsum(form, left, right, preferred_element_type=jnp.float32)


SWAP = ((0, 1), (1, 0))


def row_scores(q_part, k_rot, allowed, score_scale):
    scores = contract("qkgd,skd->kgqs", q_part, k_rot) * score_scale
    return jnp.where(allowed, scores, NEG_FILL)


def attention_forward(q_rot, k_rot, values, allowed):
    length, kv_heads, head_dim = k_rot.shape
    groups = q_rot.shape[1] // kv_heads
    score_scale = head_dim ** (-0.5)
    q_part = q_rot.reshape(length, kv_heads, groups, head_dim)
    scores = row_scores(q_part, k_rot, allowed, score_scale)
    row_peak = jnp.max(scores, axis=-1, keepdims=True)
    log_total = row_peak + jnp.log(jnp.sum(jnp.exp(scores - row_peak), axis=-1, keepdims=True))
    probs = jnp.exp(scores - log_total)
    attended = contract("kgqs,skd->qkgd", probs.astype(jnp.bfloat16), values)
    outputs = attended.reshape(length, -1).astype(jnp.bfloat16)
    return (outputs, log_total)


def attention_backward(q_rot, k_rot, values, attended, grad_attended, log_totals, allowed):
    length, kv_heads, head_dim = k_rot.shape
    groups = q_rot.shape[1] // kv_heads
    score_scale = head_dim ** (-0.5)
    q_part = q_rot.reshape(length, kv_heads, groups, head_dim)
    go_part = grad_attended.reshape(length, kv_heads, groups, head_dim)
    o_part = attended.reshape(length, kv_heads, groups, head_dim)
    scores = row_scores(q_part, k_rot, allowed, score_scale)
    probs = jnp.exp(scores - log_totals)
    weights = probs.astype(jnp.bfloat16)
    grad_values = contract("kgqs,qkgd->skd", weights, go_part)
    grad_probs = contract("qkgd,skd->kgqs", go_part, values)
    row_dots = contract("qkgd,qkgd->kgq", go_part, o_part)
    grad_scores = (probs * (grad_probs - row_dots[..., None]) * score_scale).astype(jnp.bfloat16)
    grad_queries = contract("kgqs,skd->qkgd", grad_scores, k_rot).reshape(
        length, kv_heads * groups, head_dim
    )
    grad_keys = contract("kgqs,qkgd->skd", grad_scores, q_part)
    return (grad_queries, grad_keys, grad_values)


def group_sum(partial, beside=None):
    half = partial.shape[0] // 2
    own = partial[:half] + lax.ppermute(partial[half:], "core", SWAP)
    other = lax.ppermute(own, "x_hi", SWAP)
    made = None
    if beside is not None:
        made = beside()
        other, made = lax.optimization_barrier((other, made))
    own = own + other
    total = jnp.concatenate([own, lax.ppermute(own, "core", SWAP)], axis=0)
    return total if beside is None else (total, made)


def weight_grads(pairs):
    tokens, width = pairs[0][0].shape
    lefts = []
    for left, _ in pairs:
        if not any(left is seen for seen in lefts):
            lefts.append(left)
    which = [next(i for i, seen in enumerate(lefts) if seen is left) for left, _ in pairs]
    rights = [right for _, right in pairs]
    columns = [right.shape[1] for right in rights]
    total = sum(columns)
    n_left = len(lefts)
    tile = 256
    halves = width // 2
    per_half = halves // tile

    def body(*refs):
        left_refs = refs[:n_left]
        right_refs = refs[n_left:-1]
        out_ref = refs[-1]
        start = 0
        for idx, right_ref in enumerate(right_refs):
            piece = lax.dot_general(
                left_refs[which[idx]][...],
                right_ref[...],
                (((0,), (0,)), ((), ())),
                preferred_element_type=jnp.float32,
            )
            out_ref[:, 0, :, start : start + columns[idx]] = piece.reshape(
                tile // 32, 32, columns[idx]
            )
            start += columns[idx]

    flops = 2 * tokens * width * total
    out = pl.pallas_call(
        body,
        grid=(2 * per_half,),
        in_specs=[pl.BlockSpec((tokens, tile), lambda i: (0, i)) for _ in lefts]
        + [pl.BlockSpec((tokens, c), lambda i: (0, 0)) for c in columns],
        out_specs=pl.BlockSpec(
            (tile // 32, 1, 32, total), lambda i: (i % per_half, i // per_half, 0, 0)
        ),
        out_shape=jax.ShapeDtypeStruct((width // 64, 2, 32, total), jnp.float32),
        cost_estimate=pl.CostEstimate(
            flops=flops, transcendentals=0, bytes_accessed=4 * width * total
        ),
        name="weight_grads",
    )(*lefts, *rights)
    return out.reshape(width, total)


def swap_partner_rows(part):
    rows = part.shape[0] // 2
    part = part.reshape(2, rows, part.shape[1])
    mine = lax.axis_index("x_lo")
    keep = lax.dynamic_index_in_dim(part, mine, 0, keepdims=False)
    send = lax.dynamic_index_in_dim(part, 1 - mine, 0, keepdims=False)
    return keep + lax.ppermute(send, "x_lo", SWAP)


def scatter_zy(stacked):
    return lax.psum_scatter(stacked, ("z", "y"), scatter_dimension=0, tiled=True)


def ring_scatter(block, dim, axis):
    up = [(i, (i + 1) % 4) for i in range(4)]
    down = [(i, (i - 1) % 4) for i in range(4)]
    mine = lax.axis_index(axis)

    def entry(offset):
        return lax.dynamic_index_in_dim(block, (mine + offset) % 4, dim, keepdims=False)

    far, after, before, own = (entry(2), entry(1), entry(3), entry(0))
    half = far.shape[0] // 2
    far_up = lax.ppermute(far[:half], axis, up)
    far_down = lax.ppermute(far[half:], axis, down)
    near_up = lax.ppermute(after[half:], axis, up)
    near_down = lax.ppermute(before[:half], axis, down)
    last_up = lax.ppermute(after[:half] + far_up, axis, up)
    last_down = lax.ppermute(before[half:] + far_down, axis, down)
    return jnp.concatenate(
        [own[:half] + near_down + last_up, own[half:] + near_up + last_down], axis=0
    )


def scatter_by_rings(stacked):
    width, columns = stacked.shape
    cut = columns // 2
    block = stacked.reshape(4, 4, width // 16, columns)
    first = ring_scatter(ring_scatter(block[..., :cut], 1, "y"), 0, "z")
    second = ring_scatter(ring_scatter(block[..., cut:], 0, "z"), 0, "y")
    return jnp.concatenate([first, second], axis=1)


def sum_everywhere(small):
    for axis in ("x_lo", "y", "z"):
        size = lax.axis_size(axis)
        step = 1
        while step < size:
            small = small + lax.ppermute(small, axis, [(i, i ^ step) for i in range(size)])
            step *= 2
    for axis in ("core", "x_hi"):
        small = small + lax.ppermute(small, axis, SWAP)
    return small


def layer_forward(resid, allowed, cosine, sine, params, last):
    (w_query, key_weight, value_weight, w_out, w_gate, w_up, w_down) = params[:7]
    (gain_in, gain_post, gain_query, gain_key) = params[7:]
    length = resid.shape[0]
    head_dim = gain_query.shape[0]
    scale_in = inv_rms(resid)
    normed_in = resid * scale_in
    attn_input = (normed_in * gain_in).astype(jnp.bfloat16)
    queries = jnp.dot(attn_input, w_query, preferred_element_type=jnp.float32).reshape(
        length, -1, head_dim
    )
    keys_raw = jnp.dot(attn_input, key_weight, preferred_element_type=jnp.float32).reshape(
        length, -1, head_dim
    )
    values = (
        jnp.dot(attn_input, value_weight, preferred_element_type=jnp.float32)
        .astype(jnp.bfloat16)
        .reshape(length, -1, head_dim)
    )
    q_scale = inv_rms(queries)
    q_normed = queries * q_scale
    k_scale = inv_rms(keys_raw)
    k_normed = keys_raw * k_scale
    q_rot = rotate(q_normed * gain_query, cosine, sine).astype(jnp.bfloat16)
    k_rot = rotate(k_normed * gain_key, cosine, sine).astype(jnp.bfloat16)
    attended, log_totals = attention_forward(q_rot, k_rot, values, allowed)
    attn_sum = group_sum(jnp.dot(attended, w_out, preferred_element_type=jnp.float32))
    middle = resid + attn_sum
    scale_post = inv_rms(middle)
    normed_post = middle * scale_post
    mlp_input = (normed_post * gain_post).astype(jnp.bfloat16)
    gate_logits = jnp.dot(mlp_input, w_gate, preferred_element_type=jnp.float32)
    up_pre = jnp.dot(mlp_input, w_up, preferred_element_type=jnp.float32)
    hidden = (jax.nn.silu(gate_logits) * up_pre).astype(jnp.bfloat16)
    mlp_partial = jnp.dot(hidden, w_down, preferred_element_type=jnp.float32)
    result = (middle, mlp_partial) if last else middle + group_sum(mlp_partial)
    saved = (
        scale_in,
        normed_in,
        attn_input,
        q_scale,
        q_normed,
        k_scale,
        k_normed,
        q_rot,
        k_rot,
        values,
        attended,
        log_totals,
        scale_post,
        normed_post,
        mlp_input,
        gate_logits,
        up_pre,
        hidden,
    )
    return (result, saved)


def layer_backward(upstream, saved, params, allowed, cosine, sine, carried, first):
    (w_query, key_weight, value_weight, w_out, w_gate, w_up, w_down) = params[:7]
    (gain_in, gain_post, gain_query, gain_key) = params[7:]
    (
        scale_in,
        normed_in,
        attn_input,
        q_scale,
        q_normed,
        k_scale,
        k_normed,
        q_rot,
        k_rot,
        values,
        attended,
        log_totals,
        scale_post,
        normed_post,
        mlp_input,
        gate_logits,
        up_pre,
        hidden,
    ) = saved
    length = upstream.shape[0]
    upstream_bf = upstream.astype(jnp.bfloat16)
    grad_hidden = jnp.dot(upstream_bf, w_down.T, preferred_element_type=jnp.float32)
    sigma = jax.nn.sigmoid(gate_logits)
    grad_gate_pre = (grad_hidden * up_pre * sigma * (1.0 + gate_logits * (1.0 - sigma))).astype(
        jnp.bfloat16
    )
    grad_up_pre = (grad_hidden * gate_logits * sigma).astype(jnp.bfloat16)
    mlp_partial = jnp.dot(grad_gate_pre, w_gate.T, preferred_element_type=jnp.float32) + jnp.dot(
        grad_up_pre, w_up.T, preferred_element_type=jnp.float32
    )
    mlp_pairs = [(mlp_input, grad_gate_pre), (mlp_input, grad_up_pre), (upstream_bf, hidden)]
    grad_mlp_in, mlp_grads = group_sum(mlp_partial, lambda: weight_grads(carried + mlp_pairs))
    mlp_grads = scatter_zy(mlp_grads)
    grad_gain_post = jnp.sum(mlp_partial * normed_post, axis=0)
    grad_middle = upstream + norm_back(grad_mlp_in, normed_post, scale_post, gain_post)
    middle_bf = grad_middle.astype(jnp.bfloat16)
    grad_attended = jnp.dot(middle_bf, w_out.T, preferred_element_type=jnp.float32).astype(
        jnp.bfloat16
    )
    grad_q_rot, grad_k_rot, grad_v_raw = attention_backward(
        q_rot, k_rot, values, attended, grad_attended, log_totals, allowed
    )
    grad_q_normed = rotate_back(grad_q_rot, cosine, sine)
    grad_k_normed = rotate_back(grad_k_rot, cosine, sine)
    query_gain_part = jnp.sum(grad_q_normed * q_normed, axis=(0, 1))
    key_gain_part = jnp.sum(grad_k_normed * k_normed, axis=(0, 1))
    grad_queries = (
        norm_back(grad_q_normed, q_normed, q_scale, gain_query)
        .astype(jnp.bfloat16)
        .reshape(length, -1)
    )
    grad_keys = (
        norm_back(grad_k_normed, k_normed, k_scale, gain_key)
        .astype(jnp.bfloat16)
        .reshape(length, -1)
    )
    grad_values = grad_v_raw.astype(jnp.bfloat16).reshape(length, -1)
    attn_partial = (
        jnp.dot(grad_queries, w_query.T, preferred_element_type=jnp.float32)
        + jnp.dot(grad_keys, key_weight.T, preferred_element_type=jnp.float32)
        + jnp.dot(grad_values, value_weight.T, preferred_element_type=jnp.float32)
    )
    attn_pairs = [
        (attn_input, grad_queries),
        (attn_input, grad_keys),
        (attn_input, grad_values),
        (middle_bf, attended),
    ]
    if first:
        made = weight_grads(attn_pairs)
        attn_partial, made = lax.optimization_barrier((attn_partial, made))
        attn_pairs = scatter_by_rings(made)
    grad_attn_in = group_sum(attn_partial)
    grad_gain_in = jnp.sum(attn_partial * normed_in, axis=0)
    grad_resid = grad_middle + norm_back(grad_attn_in, normed_in, scale_in, gain_in)
    gains = (grad_gain_in, grad_gain_post, query_gain_part, key_gain_part)
    return (grad_resid, mlp_grads, attn_pairs, attn_partial, gains)


def split_columns(stacked, sizes):
    pieces = []
    start = 0
    for size in sizes:
        pieces.append(stacked[:, start : start + size])
        start += size
    return pieces


def shards(
    inputs,
    segments,
    positions,
    w_query,
    key_weight,
    value_weight,
    w_out,
    w_gate,
    w_up,
    w_down,
    gain_in,
    gain_post,
    gain_query,
    gain_key,
    cotangent,
):
    all_params = (
        w_query,
        key_weight,
        value_weight,
        w_out,
        w_gate,
        w_up,
        w_down,
        gain_in,
        gain_post,
        gain_query,
        gain_key,
    )
    layer_count = w_query.shape[0]
    length = segments.shape[1]
    width = inputs.shape[1]
    half = length // 2
    core = lax.axis_index("core")

    def turn(values):
        return jnp.where(core == 0, values, jnp.concatenate([values[half:], values[:half]], axis=0))

    segment_row = turn(segments[0])
    index_row = turn(jnp.arange(length))
    allowed = (segment_row[:, None] == segment_row[None, :]) & (
        index_row[None, :] <= index_row[:, None]
    )
    cosine, sine = rope_tables(turn(positions[0]), gain_query.shape[1])
    resid = turn(inputs).astype(jnp.float32)
    saves = []
    for layer_idx in range(layer_count):
        params = tuple((member[layer_idx] for member in all_params))
        resid, saved = layer_forward(
            resid, allowed, cosine, sine, params, layer_idx == layer_count - 1
        )
        saves.append(saved)
    middle, last_partial = resid
    upstream = turn(cotangent).astype(jnp.float32)
    scattered, gains, carried = ([], [], [])
    for layer_idx in reversed(range(layer_count)):
        params = tuple((member[layer_idx] for member in all_params))
        upstream, mlp_part, attn_part, attn_partial, gain_part = layer_backward(
            upstream, saves[layer_idx], params, allowed, cosine, sine, carried, layer_idx == 0
        )
        scattered.append(mlp_part)
        carried = attn_part
        gains.insert(0, gain_part)
    scattered.append(attn_part)
    last_partial, _ = lax.optimization_barrier((last_partial, attn_partial))
    resid = middle + group_sum(last_partial)
    scattered = [swap_partner_rows(part) for part in scattered]
    sizes = [member.shape[1] for group in gains for member in [g[None] for g in group]]
    flat = sum_everywhere(
        jnp.concatenate([member for group in gains for member in group]).reshape(-1, 128)
    ).reshape(-1)
    place = lax.axis_index(("x_lo", "z", "y"))
    n_place = lax.axis_size(("x_lo", "z", "y"))
    gain_pieces = []
    start = 0
    for size in sizes:
        piece = flat[start : start + size].reshape(n_place, size // n_place)
        gain_pieces.append(lax.dynamic_index_in_dim(piece, place, 0, keepdims=False))
        start += size
    gain_out = [
        jnp.stack([gain_pieces[4 * layer_idx + member] for layer_idx in range(layer_count)])
        for member in range(4)
    ]
    mlp_sizes = [w_gate.shape[2], w_up.shape[2], w_down.shape[1]]
    attn_sizes = [w_query.shape[2], key_weight.shape[2], value_weight.shape[2], w_out.shape[1]]
    attn_split, mlp_split = ([], [])
    for step, rows in enumerate(scattered):
        sizes = (attn_sizes if step else []) + (mlp_sizes if step < layer_count else [])
        pieces = split_columns(rows, sizes)
        if step:
            attn_split.insert(0, pieces[:4])
        if step < layer_count:
            mlp_split.insert(0, pieces[-3:])
    return (
        turn(resid),
        turn(upstream),
        jnp.stack([pieces[0] for pieces in attn_split]),
        jnp.stack([pieces[1] for pieces in attn_split]),
        jnp.stack([pieces[2] for pieces in attn_split]),
        jnp.stack([pieces[3].T for pieces in attn_split]),
        jnp.stack([pieces[0] for pieces in mlp_split]),
        jnp.stack([pieces[1] for pieces in mlp_split]),
        jnp.stack([pieces[2].T for pieces in mlp_split]),
        gain_out[0],
        gain_out[1],
        gain_out[2],
        gain_out[3],
    )


def solution(mesh):
    fine = Mesh(
        mesh.devices.reshape(2, 4, 4, 2, 2), ("x_lo", "z", "y", "x_hi", "core")
    )
    dp = ("x_lo", "z", "y")
    tensor = ("x_hi", "core")
    return jax.shard_map(
        shards,
        mesh=fine,
        in_specs=(
            P(dp, None),
            P(dp, None),
            P(dp, None),
            P(None, None, tensor),
            P(None, None, tensor),
            P(None, None, tensor),
            P(None, tensor, None),
            P(None, None, tensor),
            P(None, None, tensor),
            P(None, tensor, None),
            P(),
            P(),
            P(),
            P(),
            P(dp, None),
        ),
        out_specs=(
            P(dp, None),
            P(dp, None),
            P(None, dp, tensor),
            P(None, dp, tensor),
            P(None, dp, tensor),
            P(None, tensor, dp),
            P(None, dp, tensor),
            P(None, dp, tensor),
            P(None, tensor, dp),
            P(None, dp),
            P(None, dp),
            P(None, dp),
            P(None, dp),
        ),
        check_vma=False,
    )
```
